128 devices in a mesh: dom: 64 (over x, y, z), col: 2 (over core).
Axes of the slice: x: 4, y: 4, z: 4, core: 2. Of those that a mesh axis runs over, the one named last changes fastest.
Arguments:
- adjoint_rhs: bfloat16 [12288, 105, 64], P('dom', None, 'col')
- element_blocks: bfloat16 [6144, 420, 420], P('dom', 'col')
- element_faces: int32 [6144, 4], P('dom'), may hold values from 0 to 383, as said below
- send_faces: int32 [64, 192], P('dom'), may hold values from 0 to 191
Outputs:
- second_basis: bfloat16 [12288, 105, 64], P('dom', None, 'col')
- next_vector: bfloat16 [12288, 105, 64], P('dom', None, 'col')
- hessenberg: float32 [5, 64], P(None, 'col')
The draws below stay inside these ranges and needn't reach their ends.
Inputs may be any that keep to these rules, and one draw needn't show every extreme that they name: `element_faces`: row d * 96 + e belongs to partition d. An entry below 192 is an owned face; an entry 192 + p * 3 + s stands for the face that partition p lists in send_faces at position d * 3 + s. No partition names one of its slots at or above 192 twice, and none names its own index p = d.
All inputs are finite; a program needn't handle non-finite values.
Results may differ from the reference program's by a relative error of at most 0.02.
Values may be sent and summed in bfloat16 or wider, within the bound.
A program may use at most 192 MiB of HBM per device.

```python
import math
import jax
import jax.numpy as jnp
from jax import lax

P_SIZE = 105
E_DEV = 96
F_DEV = 192
SLOT = 3
NRHS = 64
FACES = 12288
N_DOM = 64
N_COL = 2


def draw_adjoint_rhs(key, part):
    key_normal, key_rows, key_cols = jax.random.split(key, 3)
    position = jnp.arange(FACES, dtype=jnp.float32) / FACES
    row_scale = 3.0 ** position * 10.0 ** jax.random.uniform(key_rows, (FACES,), jnp.float32)
    col_scale = 10.0 ** jax.random.uniform(key_cols, (NRHS,), jnp.float32)
    normal_part = jax.random.normal(key_normal, (FACES, P_SIZE, NRHS), jnp.float32)
    return (0.3 * normal_part * row_scale[:, None, None] * col_scale[None, None, :]).astype(jnp.bfloat16)


def draw_element_blocks(key, part):
    key_noise, key_diag = jax.random.split(key)
    row_count = N_DOM * E_DEV
    block_width = 4 * P_SIZE
    noise_part = jax.random.normal(key_noise, (row_count, block_width, block_width), jnp.float32)
    diagonal = jnp.exp(jax.random.uniform(key_diag, (row_count, block_width), jnp.float32, minval=math.log(0.5), maxval=math.log(2.0)))
    identity = jnp.eye(block_width, dtype=jnp.float32)
    return (0.8 * noise_part / math.sqrt(block_width) + diagonal[:, :, None] * identity[None]).astype(jnp.bfloat16)


def draw_element_faces(key, part):
    ghosts = SLOT * N_DOM
    key_counts, key_order = jax.random.split(jax.random.fold_in(key, 17))
    counts = jax.random.randint(key_counts, (N_DOM, N_DOM), 0, SLOT + 1)
    sender = jnp.arange(N_DOM)[:, None]
    receiver = jnp.arange(N_DOM)[None, :]
    offset = (sender - receiver) % N_DOM
    forced = (offset == 1) | (offset == N_DOM - 1) | (offset == N_DOM // 2)
    counts = jnp.where(forced, SLOT, counts)
    counts = jnp.where(offset == 0, 0, counts)
    slot_index = jnp.arange(ghosts)
    in_use = slot_index[None, :] % SLOT < counts.T[:, slot_index // SLOT]
    orders = jax.vmap(lambda one_key: jax.random.permutation(one_key, 4 * E_DEV))(jax.random.split(key_order, N_DOM))
    owned_pick = jnp.where(orders < ghosts, orders, orders - ghosts) % F_DEV
    used_pick = jnp.take_along_axis(in_use, jnp.minimum(orders, ghosts - 1), axis=1) & (orders < ghosts)
    face_ids = jnp.where(used_pick, F_DEV + orders, owned_pick)
    return face_ids.reshape(N_DOM * E_DEV, 4).astype(jnp.int32)


def with_ends(values, stream_key, smallest, top_value):
    longest = values.shape.index(max(values.shape))
    spots = []
    for shift in (0, 1):
        where = [jax.random.randint(jax.random.fold_in(stream_key, axis), (), 0, length) for axis, length in enumerate(values.shape)]
        where[longest] = (where[longest] + shift) % values.shape[longest]
        spots.append(tuple(where))
    return values.at[spots[0]].set(smallest).at[spots[1]].set(top_value)


def setup_inputs(seed: int = 0) -> dict:
    keys = jax.random.split(jax.random.key(seed), 5)
    return {
        "adjoint_rhs": draw_adjoint_rhs(jax.random.fold_in(keys[4], 71), 0),
        "element_blocks": draw_element_blocks(jax.random.fold_in(keys[4], 71), 0),
        "element_faces": draw_element_faces(jax.random.fold_in(keys[4], 71), 0),
        "send_faces": with_ends(jax.random.randint(keys[3], (N_DOM, SLOT * N_DOM), 0, F_DEV), jax.random.fold_in(keys[3], 1), 0, F_DEV - 1).astype(jnp.int32),
    }


epsilon = 1e-06

def transposed(vector, element_blocks, element_faces, send_faces):
    owned_count = F_DEV
    ghosts = SLOT * N_DOM
    by_device = vector.reshape(N_DOM, owned_count, P_SIZE, NRHS)
    outgoing = jax.vmap(lambda values, chosen: values[chosen])(by_device, send_faces)
    incoming = outgoing.reshape(N_DOM, N_DOM, SLOT, P_SIZE, NRHS).transpose(1, 0, 2, 3, 4).reshape(N_DOM, ghosts, P_SIZE, NRHS)
    known_traces = jnp.concatenate([by_device, incoming], axis=1)
    matrices = element_blocks.reshape(N_DOM, E_DEV, 4 * P_SIZE, 4 * P_SIZE)
    face_table = element_faces.reshape(N_DOM, E_DEV, 4)
    slot_share = 4 // N_COL

    def device_terms(operands):
        values, blocks_here, faces_here = operands
        picked = values[faces_here].reshape(E_DEV, 4 * P_SIZE, NRHS)
        totals = jnp.zeros((owned_count + ghosts, P_SIZE, NRHS), jnp.float32)
        for column in range(N_COL):
            first_row = column * slot_share * P_SIZE
            last_row = first_row + slot_share * P_SIZE
            partial_terms = jnp.einsum('ekb,ekr->ebr', blocks_here[:, first_row:last_row].astype(jnp.float32), picked[:, first_row:last_row].astype(jnp.float32))
            summed = jax.ops.segment_sum(partial_terms.reshape(E_DEV * 4, P_SIZE, NRHS), faces_here.reshape(-1), num_segments=owned_count + ghosts)
            totals = totals + lax.optimization_barrier(summed.astype(jnp.bfloat16)).astype(jnp.float32)
        return totals
    totals = lax.map(device_terms, (known_traces, matrices, face_table))
    returned = totals[:, owned_count:].reshape(N_DOM, N_DOM, SLOT, P_SIZE, NRHS).transpose(1, 0, 2, 3, 4).reshape(N_DOM, ghosts, P_SIZE, NRHS)
    added = jax.vmap(lambda pieces, chosen: jax.ops.segment_sum(pieces, chosen, num_segments=owned_count))(returned, send_faces)
    return (totals[:, :owned_count] + added).reshape(N_DOM * owned_count, P_SIZE, NRHS)

def reference(adjoint_rhs, element_blocks, element_faces, send_faces):
    entries = FACES * P_SIZE
    residual = adjoint_rhs.astype(jnp.float32)
    start_norm = jnp.sqrt(lax.optimization_barrier(jnp.sum(residual * residual, axis=(0, 1))) / entries + epsilon)
    first_basis = (residual / start_norm).astype(jnp.bfloat16)
    first_image = transposed(first_basis, element_blocks, element_faces, send_faces)
    first_float = first_basis.astype(jnp.float32)
    diagonal_term = lax.optimization_barrier(jnp.sum(first_float * first_image, axis=(0, 1))) / entries
    projected = first_image - diagonal_term * first_float
    next_norm = jnp.sqrt(lax.optimization_barrier(jnp.sum(projected * projected, axis=(0, 1))) / entries + epsilon)
    second_basis = (projected / next_norm).astype(jnp.bfloat16)
    second_image = transposed(second_basis, element_blocks, element_faces, send_faces)
    second_float = second_basis.astype(jnp.float32)
    proj_first = lax.optimization_barrier(jnp.sum(first_float * second_image, axis=(0, 1))) / entries
    proj_second = lax.optimization_barrier(jnp.sum(second_float * second_image, axis=(0, 1))) / entries
    next_vector = (second_image - proj_first * first_float - proj_second * second_float).astype(jnp.bfloat16)
    hessenberg = jnp.stack([start_norm, diagonal_term, next_norm, proj_first, proj_second])
    return (second_basis, next_vector, hessenberg)
```

```python
import jax
import jax.numpy as jnp
from jax import lax
from jax.experimental import pallas as pl
from jax.experimental.pallas import tpu as pltpu
from jax.sharding import PartitionSpec as P

P_SIZE = 105
EPS = 1e-06
MESH = pl.DeviceIdType.MESH
NDOM = 64
ELEMS = 96
OWNED = 192
SLOT = 3
HALF = 32
WIRE = 80
STEP = 27
ENTRIES = float(NDOM * OWNED * P_SIZE)
F32 = jnp.float32
BF16 = jnp.bfloat16
VMEM_LIMIT = 60000 * 1024


def lanes(rows):
    return lax.broadcasted_iota(jnp.int32, (rows, 128), 1)


def rows_of(rows):
    return lax.broadcasted_iota(jnp.int32, (rows, 128), 0)


def pack(f0, f1, f2):
    lane = lanes(16)
    tail = f2[16:]
    out = []
    for j, part in enumerate((f0[:16], f0[16:], f1[:16], f1[16:], f2[:16])):
        moved = pltpu.roll(tail, 105 - 21 * j, 1)
        out.append(jnp.where(lane < 105, part, jnp.where(lane < 126, moved, 0.0)))
    return jnp.concatenate(out, axis=0)


def unpack(message):
    lane = lanes(16)
    tail = jnp.zeros((16, 128), F32)
    parts = []
    for j in range(5):
        part = message[16 * j : 16 * j + 16]
        moved = pltpu.roll(part, 128 - (105 - 21 * j), 1)
        tail = jnp.where((lane >= 21 * j) & (lane < 21 * j + 21), moved, tail)
        parts.append(jnp.where(lane < 105, part, 0.0))
    cat = lambda a, b: jnp.concatenate([a, b], axis=0)
    return cat(parts[0], parts[1]), cat(parts[2], parts[3]), cat(parts[4], tail)


def to_lanes(column):
    return jnp.sum(jnp.where(rows_of(HALF) == lanes(HALF), column, 0.0), axis=0, keepdims=True)


def to_rows(row):
    return jnp.sum(jnp.where(rows_of(HALF) == lanes(HALF), row, 0.0), axis=1, keepdims=True)


def lane_sum(x):
    return jnp.sum(x, axis=1, keepdims=True)


def relayout_kernel(a_ref, o_ref):
    group = a_ref.shape[1]
    for s in range(2):
        for k in range(0, 105, 16):
            n = min(16, 105 - k)
            x = a_ref[s * 105 + k : s * 105 + k + n]
            if n < 16:
                x = jnp.concatenate([x, jnp.zeros((16 - n, group, 420), x.dtype)], 0)
            y = jnp.swapaxes(x, 0, 1)
            for b in range(4):
                z = jnp.concatenate(
                    [y[:, :, 105 * b : 105 * b + 105], jnp.zeros((group, 16, 23), y.dtype)], -1
                )
                o_ref[:, s * 128 + k : s * 128 + k + 16, b * 128 : b * 128 + 128] = z
        o_ref[:, s * 128 + 112 : s * 128 + 128, :] = jnp.zeros((group, 16, 512), o_ref.dtype)


def relayout(blocks):
    group = 16
    return pl.pallas_call(
        relayout_kernel,
        grid=(ELEMS // group,),
        in_specs=[pl.BlockSpec((210, group, 420), lambda i: (0, i, 0))],
        out_specs=pl.BlockSpec((group, 256, 512), lambda i: (i, 0, 0)),
        out_shape=jax.ShapeDtypeStruct((ELEMS, 256, 512), BF16),
        compiler_params=pltpu.CompilerParams(vmem_limit_bytes=VMEM_LIMIT),
    )(blocks)


def pack_faces(send_ref, face, out_ref):
    def step(p, _):
        out_ref[p] = pack(*(face(send_ref[SLOT * p + s]) for s in range(SLOT))).astype(BF16)
        return 0

    lax.fori_loop(0, NDOM, step, 0, unroll=2)


def start_kernel(send_ref, r_ref, full_ref, out_ref, stat_ref):
    mask = lanes(HALF) < P_SIZE

    def step(f, total):
        x = r_ref[f].astype(F32)
        x = jnp.concatenate([x, jnp.zeros((HALF, 23), F32)], 1)
        full_ref[f] = x.astype(BF16)
        return total + x * x

    total = lax.fori_loop(0, OWNED, step, jnp.zeros((HALF, 128), F32), unroll=4)
    del mask
    stat_ref[...] = jnp.zeros((8, 128), F32)
    stat_ref[0:1] = to_lanes(lane_sum(total))
    pack_faces(send_ref, lambda f: full_ref[f].astype(F32), out_ref)


def start(send, r):
    return pl.pallas_call(
        start_kernel,
        in_specs=[pl.BlockSpec(memory_space=pltpu.SMEM), pl.BlockSpec(memory_space=pltpu.VMEM)],
        out_specs=[pl.BlockSpec(memory_space=pltpu.VMEM)] * 3,
        out_shape=[
            jax.ShapeDtypeStruct((OWNED, HALF, 128), BF16),
            jax.ShapeDtypeStruct((NDOM, WIRE, 128), BF16),
            jax.ShapeDtypeStruct((8, 128), F32),
        ],
        compiler_params=pltpu.CompilerParams(vmem_limit_bytes=VMEM_LIMIT),
    )(send, r)


def apply_kernel(
    faces_ref, prev_ref, last_ref, own_ref, partner_ref, ghost_ref, ghost2_ref, a_ref,
    keep_ref, give_ref, keepg_ref, giveg_ref, known_ref, sums_ref,
):
    i = pl.program_id(0)
    group = a_ref.shape[0]
    first = 2 * lax.axis_index("col")

    @pl.when(i == 0)
    def _():
        def put(f, _):
            known_ref[f, :HALF] = own_ref[f]
            known_ref[f, HALF:] = partner_ref[f]
            return 0

        lax.fori_loop(0, OWNED, put, 0, unroll=4)

        def put_ghost(p, _):
            for half, source in enumerate((ghost_ref, ghost2_ref)):
                for s, face in enumerate(unpack(source[p].astype(F32))):
                    known_ref[OWNED + SLOT * p + s, half * HALF : half * HALF + HALF] = face.astype(
                        BF16
                    )
            return 0

        lax.fori_loop(0, NDOM, put_ghost, 0, unroll=2)
        sums_ref[4 * ELEMS] = jnp.zeros((2 * HALF, 128), F32)

    for e in range(group):
        at = 4 * (i * group + e)
        x = jnp.concatenate(
            [known_ref[faces_ref[at + first]], known_ref[faces_ref[at + first + 1]]], axis=1
        )
        y = jnp.dot(x, a_ref[e], preferred_element_type=F32)
        for b in range(4):
            sums_ref[at + b] = y[:, 128 * b : 128 * b + 128] + sums_ref[prev_ref[at + b]]

    @pl.when(i == pl.num_programs(0) - 1)
    def _():
        def take(f, _):
            total = sums_ref[last_ref[f]].astype(BF16)
            keep_ref[f] = total[:HALF]
            give_ref[f] = total[HALF:]
            return 0

        lax.fori_loop(0, OWNED, take, 0, unroll=4)

        def take_ghost(p, _):
            t = [sums_ref[last_ref[OWNED + SLOT * p + s]] for s in range(SLOT)]
            keepg_ref[p] = pack(*(x[:HALF] for x in t)).astype(BF16)
            giveg_ref[p] = pack(*(x[HALF:] for x in t)).astype(BF16)
            return 0

        lax.fori_loop(0, NDOM, take_ghost, 0, unroll=2)


def whole(shape):
    return pl.BlockSpec(shape, lambda i: (0,) * len(shape), pipeline_mode=pl.Buffered(1))


def apply(faces, prev, last, own, partner, ghost, ghost2, blocks):
    group = 8
    owned, wire = (OWNED, HALF, 128), (NDOM, WIRE, 128)
    return pl.pallas_call(
        apply_kernel,
        grid=(ELEMS // group,),
        in_specs=[pl.BlockSpec(memory_space=pltpu.SMEM)] * 3
        + [whole(owned), whole(owned), whole(wire), whole(wire)]
        + [pl.BlockSpec((group, 256, 512), lambda i: (i, 0, 0))],
        out_specs=[whole(owned), whole(owned), whole(wire), whole(wire)],
        out_shape=[jax.ShapeDtypeStruct(s, BF16) for s in (owned, owned, wire, wire)],
        scratch_shapes=[
            pltpu.VMEM((2 * OWNED, 2 * HALF, 128), BF16),
            pltpu.VMEM((4 * ELEMS + 1, 2 * HALF, 128), F32),
        ],
        compiler_params=pltpu.CompilerParams(vmem_limit_bytes=VMEM_LIMIT),
    )(faces, prev, last, own, partner, ghost, ghost2, blocks)


def add_returned(prev_ref, last_ref, ret_ref, keep_ref, got_ref, v_ref, image):
    v_ref[OWNED] = jnp.zeros((HALF, 128), F32)

    def step(p, _):
        for s, face in enumerate(unpack(ret_ref[p].astype(F32))):
            at = SLOT * p + s
            v_ref[at] = face + v_ref[prev_ref[at]]
        return 0

    lax.fori_loop(0, NDOM, step, 0, unroll=2)

    def own(f, carry):
        value = keep_ref[f].astype(F32) + got_ref[f].astype(F32) + v_ref[last_ref[f]]
        return image(f, value, carry)

    zero = jnp.zeros((HALF, 128), F32)
    return lax.fori_loop(0, OWNED, own, (zero, zero), unroll=4)


def start_norm_of(stat_ref):
    total = jnp.sum(stat_ref[:, 0, :], axis=0, keepdims=True)
    return jnp.sqrt(total / ENTRIES + EPS)


def first_kernel(
    prev_ref, last_ref, ret_ref, keep_ref, got_ref, r_ref, stat_ref,
    u_ref, b_ref, out_ref, v_ref,
):
    norm = to_rows(start_norm_of(stat_ref))

    def image(f, value, carry):
        bb, bu = carry
        u = value / norm
        b = (r_ref[f].astype(F32) / norm).astype(BF16)
        u_ref[f] = u
        b_ref[f] = b
        b = b.astype(F32)
        return bb + b * b, bu + b * u

    bb, bu = add_returned(prev_ref, last_ref, ret_ref, keep_ref, got_ref, v_ref, image)
    bb, bu = lane_sum(bb), lane_sum(bu)
    local = bu / jnp.where(bb > 0.0, bb, 1.0)

    def square(f, total):
        off = u_ref[f] - local * b_ref[f].astype(F32)
        return total + off * off

    rest = lax.fori_loop(0, OWNED, square, jnp.zeros((HALF, 128), F32), unroll=4)
    out_ref[...] = jnp.zeros((8, 128), F32)
    for row, x in enumerate((bb, bu, lane_sum(rest))):
        out_ref[row : row + 1] = to_lanes(x)


def projections(stat_ref):
    bb, bu, rest = stat_ref[:, 0, :], stat_ref[:, 1, :], stat_ref[:, 2, :]
    diagonal = jnp.sum(bu, axis=0, keepdims=True) / ENTRIES
    local = bu / jnp.where(bb > 0.0, bb, 1.0)
    off = local - diagonal
    squares = jnp.sum(rest + off * off * bb, axis=0, keepdims=True)
    return diagonal, jnp.sqrt(squares / ENTRIES + EPS)


def basis_kernel(send_ref, stat_ref, u_ref, b_ref, b2_ref, out_ref, coef_ref):
    diagonal, norm = projections(stat_ref)
    coef_ref[...] = jnp.zeros((8, 128), F32)
    coef_ref[0:1] = diagonal
    coef_ref[1:2] = norm
    d, n = to_rows(diagonal), to_rows(norm)

    def step(f, _):
        b2_ref[f] = ((u_ref[f] - d * b_ref[f].astype(F32)) / n).astype(BF16)
        return 0

    lax.fori_loop(0, OWNED, step, 0, unroll=4)
    pack_faces(send_ref, lambda f: b2_ref[f].astype(F32), out_ref)


def second_kernel(
    prev_ref, last_ref, ret_ref, keep_ref, got_ref, b_ref, b2_ref,
    w_ref, out_ref, v_ref,
):
    def image(f, value, carry):
        one, two = carry
        w_ref[f] = value
        return one + b_ref[f].astype(F32) * value, two + b2_ref[f].astype(F32) * value

    one, two = add_returned(prev_ref, last_ref, ret_ref, keep_ref, got_ref, v_ref, image)
    out_ref[...] = jnp.zeros((8, 128), F32)
    out_ref[0:1] = to_lanes(lane_sum(one))
    out_ref[1:2] = to_lanes(lane_sum(two))


def final_kernel(first_ref, coef_ref, stat_ref, w_ref, b_ref, b2_ref, basis_ref, next_ref, h_ref):
    one = jnp.sum(stat_ref[:, 0, :], axis=0, keepdims=True) / ENTRIES
    two = jnp.sum(stat_ref[:, 1, :], axis=0, keepdims=True) / ENTRIES
    rows = (start_norm_of(first_ref), coef_ref[0:1], coef_ref[1:2], one, two)
    for i, row in enumerate(rows):
        h_ref[i : i + 1] = row[:, :HALF]
    p1, p2 = to_rows(one), to_rows(two)

    def step(f, _):
        b2 = b2_ref[f]
        out = w_ref[f] - p1 * b_ref[f].astype(F32) - p2 * b2.astype(F32)
        next_ref[f] = out[:, :P_SIZE].astype(BF16)
        basis_ref[f] = b2[:, :P_SIZE]
        return 0

    lax.fori_loop(0, OWNED, step, 0, unroll=4)


def local(kernel, scalars, arrays, outs, scratch=()):
    return pl.pallas_call(
        kernel,
        in_specs=[pl.BlockSpec(memory_space=pltpu.SMEM)] * len(scalars)
        + [pl.BlockSpec(memory_space=pltpu.VMEM)] * len(arrays),
        out_specs=[pl.BlockSpec(memory_space=pltpu.VMEM)] * len(outs),
        out_shape=[jax.ShapeDtypeStruct(s, t) for s, t in outs],
        scratch_shapes=list(scratch),
        compiler_params=pltpu.CompilerParams(vmem_limit_bytes=VMEM_LIMIT),
    )(*scalars, *arrays)


def greet(d, c, partner):
    barrier = pltpu.get_barrier_semaphore()

    def signal(k, _):
        pl.semaphore_signal(
            barrier, inc=1, device_id=(lax.rem(d + k, NDOM), c), device_id_type=MESH
        )
        return 0

    lax.fori_loop(1, NDOM, signal, 0)
    if partner:
        pl.semaphore_signal(barrier, inc=1, device_id=(d, 1 - c), device_id_type=MESH)
    pl.semaphore_wait(barrier, NDOM if partner else NDOM - 1)


def offset(k):
    return lax.rem(k * STEP, NDOM)


def each(body):
    def step(k, _):
        body(k)
        return 0

    lax.fori_loop(1, NDOM, step, 0)


def remote(source, target, send, recv, d, c):
    return pltpu.make_async_remote_copy(
        source, target, send, recv, device_id=(d, c), device_id_type=MESH
    )


def spread_stats(stat, stats, stage, send, recv, sem, d, c):
    mine = pltpu.make_async_copy(stat, stats.at[d], sem)
    mine.start()

    def copy(k):
        return remote(
            stat, stats.at[d], send.at[k], recv.at[k], lax.rem(d + offset(k), NDOM), c
        )

    each(lambda k: copy(k).start())
    return mine, copy


def halo_kernel(
    wire, own, stat, ghost, ghost2, partner, stats,
    send, recv, fsend, frecv, ssend, srecv, own_sem, stat_sem,
):
    d, c = lax.axis_index("dom"), lax.axis_index("col")
    greet(d, c, True)
    mine, stat_copy = spread_stats(stat, stats, 0, ssend, srecv, stat_sem, d, c)
    across = remote(own, partner, own_sem.at[0], own_sem.at[1], d, 1 - c)
    across.start()

    def copy(k):
        t = lax.rem(d + offset(k), NDOM)
        return remote(wire.at[t], ghost.at[d], send.at[k], recv.at[k], t, c)

    def forward(k):
        s = lax.rem(d - offset(k) + NDOM, NDOM)
        return remote(ghost.at[s], ghost2.at[s], fsend.at[k], frecv.at[k], d, 1 - c)

    each(lambda k: copy(k).start())

    def arrive(k):
        copy(k).wait_recv()
        forward(k).start()

    each(arrive)

    def finish(k):
        copy(k).wait_send()
        forward(k).wait()
        stat_copy(k).wait()

    each(finish)
    across.wait()
    mine.wait()


def sems(n):
    return pltpu.SemaphoreType.DMA((n,))


def halo(wire, own, stat):
    return pl.pallas_call(
        halo_kernel,
        in_specs=[pl.BlockSpec(memory_space=pl.ANY)] * 3,
        out_specs=[pl.BlockSpec(memory_space=pl.ANY)] * 4,
        out_shape=[
            jax.ShapeDtypeStruct((NDOM, WIRE, 128), BF16),
            jax.ShapeDtypeStruct((NDOM, WIRE, 128), BF16),
            jax.ShapeDtypeStruct((OWNED, HALF, 128), BF16),
            jax.ShapeDtypeStruct((NDOM, 8, 128), F32),
        ],
        scratch_shapes=[sems(NDOM)] * 6 + [sems(2), pltpu.SemaphoreType.DMA],
        compiler_params=pltpu.CompilerParams(collective_id=0, has_side_effects=True),
    )(wire, own, stat)


PARTS = 8


def give_back_kernel(
    keepg, giveg, give, got, ret, gotg, total, send, recv, xsend, xrecv, own_sem
):
    d, c = lax.axis_index("dom"), lax.axis_index("col")
    greet(d, c, True)
    size = NDOM // PARTS

    def cross(i):
        part = pl.ds(i * size, size)
        return remote(giveg.at[part], gotg.at[part], xsend.at[i], xrecv.at[i], d, 1 - c)

    for i in range(PARTS):
        cross(i).start()
    across = remote(give, got, own_sem.at[0], own_sem.at[1], d, 1 - c)
    across.start()

    def add(i, _):
        cross(i).wait_recv()
        for j in range(size):
            at = i * size + j
            total[at] = (keepg[at].astype(F32) + gotg[at].astype(F32)).astype(BF16)
        return 0

    lax.fori_loop(0, PARTS, add, 0)

    def copy(k):
        t = lax.rem(d + offset(k), NDOM)
        return remote(total.at[t], ret.at[d], send.at[k], recv.at[k], t, c)

    each(lambda k: copy(k).start())
    each(lambda k: copy(k).wait())
    for i in range(PARTS):
        cross(i).wait_send()
    across.wait()


def give_back(keepg, giveg, give):
    wire = (NDOM, WIRE, 128)
    return pl.pallas_call(
        give_back_kernel,
        in_specs=[pl.BlockSpec(memory_space=pltpu.VMEM)]
        + [pl.BlockSpec(memory_space=pl.ANY)] * 2,
        out_specs=[pl.BlockSpec(memory_space=pl.ANY)] * 2,
        out_shape=[
            jax.ShapeDtypeStruct((OWNED, HALF, 128), BF16),
            jax.ShapeDtypeStruct(wire, BF16),
        ],
        scratch_shapes=[pltpu.VMEM(wire, BF16), pltpu.VMEM(wire, BF16)]
        + [sems(NDOM), sems(NDOM), sems(PARTS), sems(PARTS), sems(2)],
        compiler_params=pltpu.CompilerParams(
            collective_id=1, has_side_effects=True, vmem_limit_bytes=VMEM_LIMIT
        ),
    )(keepg, giveg, give)


def stats_kernel(stat, stats, send, recv, sem):
    d, c = lax.axis_index("dom"), lax.axis_index("col")
    greet(d, c, False)
    mine, copy = spread_stats(stat, stats, 0, send, recv, sem, d, c)
    each(lambda k: copy(k).wait())
    mine.wait()


def spread(stat):
    return pl.pallas_call(
        stats_kernel,
        in_specs=[pl.BlockSpec(memory_space=pltpu.VMEM)],
        out_specs=pl.BlockSpec(memory_space=pltpu.VMEM),
        out_shape=jax.ShapeDtypeStruct((NDOM, 8, 128), F32),
        scratch_shapes=[sems(NDOM), sems(NDOM), pltpu.SemaphoreType.DMA],
        compiler_params=pltpu.CompilerParams(collective_id=2, has_side_effects=True),
    )(stat)


def latest(names, queries, before, usable, empty):
    j = jnp.arange(names.shape[0], dtype=jnp.int32)
    match = (names[None, :] == queries[:, None]) & (j[None, :] < before[:, None]) & usable[None, :]
    best = jnp.max(jnp.where(match, j[None, :], -1), axis=1)
    return jnp.where(best < 0, empty, best)


def body(adjoint_rhs, element_blocks, element_faces, send_faces):
    d = lax.axis_index("dom")
    faces = element_faces.reshape(-1)
    send = send_faces[0]
    slots = jnp.arange(2 * OWNED, dtype=jnp.int32)
    at = jnp.arange(faces.shape[0], dtype=jnp.int32)
    full = jnp.full((2 * OWNED,), 2 * OWNED, jnp.int32)
    every = jnp.ones((faces.shape[0],), bool)
    found = latest(
        faces, jnp.concatenate([faces, slots]), jnp.concatenate([at, full]), every, 4 * ELEMS
    )
    prev, last = found[: 4 * ELEMS], found[4 * ELEMS :]
    owned = slots[:OWNED]
    other = owned // SLOT != d
    found2 = latest(
        send, jnp.concatenate([send, owned]), jnp.concatenate([owned, full[:OWNED]]), other, OWNED
    )
    prev2, last2 = found2[:OWNED], found2[OWNED:]

    blocks = relayout(jnp.transpose(element_blocks, (1, 0, 2)))
    shape = (OWNED, HALF, 128)
    r, wire, stat = start(send, jnp.transpose(adjoint_rhs, (0, 2, 1)))

    def transposed(wire, own, stat):
        ghost, ghost2, partner, stats = halo(wire, own, stat)
        keep, give, keepg, giveg = apply(
            faces, prev, last, own, partner, ghost, ghost2, blocks
        )
        got, ret = give_back(keepg, giveg, give)
        return (ret, keep, got), stats

    scratch = [pltpu.VMEM((OWNED + 1, HALF, 128), F32)]
    parts, stats0 = transposed(wire, r, stat)
    u, b1, stat = local(
        first_kernel, (prev2, last2), (*parts, r, stats0),
        [(shape, F32), (shape, BF16), ((8, 128), F32)], scratch,
    )
    stats1 = spread(stat)
    b2, wire, coef = local(
        basis_kernel, (send,), (stats1, u, b1),
        [(shape, BF16), ((NDOM, WIRE, 128), BF16), ((8, 128), F32)],
    )
    parts, _ = transposed(wire, b2, coef)
    w, stat = local(
        second_kernel, (prev2, last2), (*parts, b1, b2),
        [(shape, F32), ((8, 128), F32)], scratch,
    )
    stats2 = spread(stat)
    out = (OWNED, HALF, P_SIZE)
    basis, vector, hessenberg = local(
        final_kernel, (), (stats0, coef, stats2, w, b1, b2),
        [(out, BF16), (out, BF16), ((5, HALF), F32)],
    )
    swap = lambda x: jnp.transpose(x, (0, 2, 1))
    return swap(basis), swap(vector), hessenberg


def solution(mesh):
    in_specs = (P("dom", None, "col"), P("dom", "col", None), P("dom", None), P("dom", None))
    out_specs = (P("dom", None, "col"), P("dom", None, "col"), P(None, "col"))
    return jax.shard_map(body, mesh=mesh, in_specs=in_specs, out_specs=out_specs, check_vma=False)
```

```python
import jax
import jax.numpy as jnp
from jax import lax
from jax.experimental import pallas as pl
from jax.experimental.pallas import tpu as pltpu
from jax.sharding import PartitionSpec as P

P_SIZE = 105
EPS = 1e-06
MESH = pl.DeviceIdType.MESH
NDOM = 64
ELEMS = 96
OWNED = 192
SLOT = 3
HALF = 32
WIRE = 80
STEP = 27
ENTRIES = float(NDOM * OWNED * P_SIZE)
F32 = jnp.float32
BF16 = jnp.bfloat16
VMEM_LIMIT = 67043328
GROUP = 8
PARTS = 8


def lanes(rows):
    return lax.broadcasted_iota(jnp.int32, (rows, 128), 1)


def rows_of(rows):
    return lax.broadcasted_iota(jnp.int32, (rows, 128), 0)


def pack(f0, f1, f2):
    lane = lanes(16)
    tail = f2[16:]
    out = []
    for j, part in enumerate((f0[:16], f0[16:], f1[:16], f1[16:], f2[:16])):
        moved = pltpu.roll(tail, 105 - 21 * j, 1)
        out.append(jnp.where(lane < 105, part, jnp.where(lane < 126, moved, 0.0)))
    return jnp.concatenate(out, axis=0)


def unpack(message):
    lane = lanes(16)
    tail = jnp.zeros((16, 128), F32)
    parts = []
    for j in range(5):
        part = message[16 * j : 16 * j + 16]
        moved = pltpu.roll(part, 128 - (105 - 21 * j), 1)
        tail = jnp.where((lane >= 21 * j) & (lane < 21 * j + 21), moved, tail)
        parts.append(jnp.where(lane < 105, part, 0.0))
    cat = lambda a, b: jnp.concatenate([a, b], axis=0)
    return cat(parts[0], parts[1]), cat(parts[2], parts[3]), cat(parts[4], tail)


def to_lanes(column):
    return jnp.sum(jnp.where(rows_of(HALF) == lanes(HALF), column, 0.0), axis=0, keepdims=True)


def to_rows(row):
    return jnp.sum(jnp.where(rows_of(HALF) == lanes(HALF), row, 0.0), axis=1, keepdims=True)


def lane_sum(x):
    return jnp.sum(x, axis=1, keepdims=True)


def relayout(a, o_ref, e0):
    group = GROUP
    at = pl.ds(e0, group)
    for s in range(2):
        for k in range(0, 105, 16):
            n = min(16, 105 - k)
            x = a[s * 105 + k : s * 105 + k + n]
            if n < 16:
                x = jnp.concatenate([x, jnp.zeros((16 - n, group, 420), x.dtype)], 0)
            y = jnp.swapaxes(x, 0, 1)
            for b in range(4):
                z = jnp.concatenate(
                    [y[:, :, 105 * b : 105 * b + 105], jnp.zeros((group, 16, 23), y.dtype)], -1
                )
                o_ref[at, s * 128 + k : s * 128 + k + 16, b * 128 : b * 128 + 128] = z
        o_ref[at, s * 128 + 112 : s * 128 + 128, :] = jnp.zeros((group, 16, 512), o_ref.dtype)


def offset(k):
    return lax.rem(k * STEP, NDOM)


def loop(first, last, body, unroll=1):
    def step(k, _):
        body(k)
        return 0

    lax.fori_loop(first, last, step, 0, unroll=unroll)


def each(body, unroll=1):
    loop(1, NDOM, body, unroll)


def remote(source, target, send, recv, d, c):
    return pltpu.make_async_remote_copy(
        source, target, send, recv, device_id=(d, c), device_id_type=MESH
    )


def to_f32(x):
    return x.astype(F32)


def whole_kernel(
    send_ref, faces_ref, prev_ref, last_ref, prev2_ref, last2_ref, r_ref, a_hbm,
    basis_hbm, next_hbm, h_ref,
    blocks, known, sums, b1, wire, ghost, ghost2, keep, give, got, keepg, giveg, gotg, ret,
    stat, stats, staging,
    a_sem, hsend, hrecv, fsend, frecv, ssend, srecv, xsend, xrecv, rsend, rrecv, pair_sem, sem,
):
    d, c = lax.axis_index("dom"), lax.axis_index("col")
    other = 1 - c
    low, high = pl.ds(0, HALF), pl.ds(HALF, HALF)
    owned = pl.ds(0, OWNED)
    zero = jnp.zeros((HALF, 128), F32)

    def target(k):
        return lax.rem(d + offset(k), NDOM)

    def source(k):
        return lax.rem(d - offset(k) + NDOM, NDOM)

    def load(g):
        slot = lax.rem(g, 2)
        part = a_hbm.at[:, pl.ds(pl.multiple_of(g * GROUP, GROUP), GROUP), :]
        return pltpu.make_async_copy(part, staging.at[slot], a_sem.at[slot])

    def stat_copy(i, k):
        return remote(stat, stats.at[i, d], ssend.at[k], srecv.at[k], target(k), c)

    def spread(i):
        mine = pltpu.make_async_copy(stat, stats.at[i, d], sem.at[0])
        mine.start()
        each(lambda k: stat_copy(i, k).start())
        mine.wait()

    def gathered(i):
        each(lambda k: stat_copy(i, k).wait())

    def send_copy(k):
        return remote(wire.at[target(k)], ghost.at[d], hsend.at[k], hrecv.at[k], target(k), c)

    def forward(k):
        s = source(k)
        return remote(ghost.at[s], ghost2.at[s], fsend.at[k], frecv.at[k], d, other)

    def across():
        return remote(
            known.at[owned, low], known.at[owned, high], pair_sem.at[0], pair_sem.at[1], d, other
        )

    def cross(i):
        part = pl.ds(i * (NDOM // PARTS), NDOM // PARTS)
        return remote(giveg.at[part], gotg.at[part], xsend.at[i], xrecv.at[i], d, other)

    def give_copy():
        return remote(give, got, pair_sem.at[2], pair_sem.at[3], d, other)

    def back(k):
        return remote(keepg.at[k], ret.at[d], rsend.at[k], rrecv.at[k], target(k), c)

    def pack_faces(face):
        def step(p):
            faces = [face(send_ref[SLOT * p + s]) for s in range(SLOT)]
            wire[p] = pack(*faces).astype(BF16)

        loop(0, NDOM, step, 4)

    def fill(s, source_ref, half):
        for j, face in enumerate(unpack(to_f32(source_ref[s]))):
            known[OWNED + SLOT * s + j, half * HALF : half * HALF + HALF] = face.astype(BF16)

    def arrive(k):
        send_copy(k).wait_recv()
        forward(k).start()
        fill(source(k), ghost, 0)

    def halo_end():
        def step(k):
            forward(k).wait_recv()
            fill(source(k), ghost2, 1)

        each(step, 3)

        def done(k):
            send_copy(k).wait_send()
            forward(k).wait_send()

        each(done)
        across().wait()

    def apply():
        first = 2 * c
        sums[4 * ELEMS] = jnp.zeros((2 * HALF, 128), F32)

        def element(e):
            at = 4 * e
            x = jnp.concatenate(
                [known[faces_ref[at + first]], known[faces_ref[at + first + 1]]], axis=1
            )
            y = jnp.dot(x, blocks[e], preferred_element_type=F32)
            for b in range(4):
                sums[at + b] = y[:, 128 * b : 128 * b + 128] + sums[prev_ref[at + b]]

        loop(0, ELEMS, element, 8)
        size = NDOM // PARTS

        def part(i):
            def one(j):
                k = i * size + j
                p = target(k)
                t = [sums[last_ref[OWNED + SLOT * p + s]] for s in range(SLOT)]
                keepg[k] = pack(*(x[:HALF] for x in t)).astype(BF16)
                giveg[k] = pack(*(x[HALF:] for x in t)).astype(BF16)

            loop(0, size, one, 4)

            @pl.when(i > 0)
            def _():
                cross(i - 1).start()

        loop(0, PARTS, part)

        def take(f):
            total = sums[last_ref[f]].astype(BF16)
            keep[f] = total[:HALF]
            give[f] = total[HALF:]

        loop(0, OWNED, take, 8)
        cross(PARTS - 1).start()
        give_copy().start()

        def pass_on(i):
            cross(i).wait_recv()

            def one(j):
                k = i * size + j
                keepg[k] = (to_f32(keepg[k]) + to_f32(gotg[k])).astype(BF16)

            loop(0, size, one, 4)

            def go(j):
                @pl.when(i + j > 0)
                def _():
                    back(i * size + j).start()

            loop(0, size, go)

        loop(0, PARTS, pass_on)

    def add_returned(image):
        give_copy().wait()
        loop(0, PARTS, lambda i: cross(i).wait_send())
        each(lambda k: back(k).wait())
        sums[OWNED, :HALF] = zero

        def step(p):
            for s, face in enumerate(unpack(to_f32(ret[p]))):
                at = SLOT * p + s
                sums[at, :HALF] = face + sums[prev2_ref[at], :HALF]

        loop(0, NDOM, step, 4)

        def own(f, carry):
            value = to_f32(keep[f]) + to_f32(got[f]) + sums[last2_ref[f], :HALF]
            return image(f, value, carry)

        return lax.fori_loop(0, OWNED, own, (zero, zero), unroll=8)

    def stat_rows(*columns):
        stat[...] = jnp.zeros((8, 128), F32)
        for row, x in enumerate(columns):
            stat[row : row + 1] = to_lanes(lane_sum(x))

    def stat_of(i, row):
        return stats[i, :, row, :]

    def total_of(i, row):
        return jnp.sum(stat_of(i, row), axis=0, keepdims=True)

    load(0).start()
    load(1).start()
    barrier = pltpu.get_barrier_semaphore()
    each(
        lambda k: pl.semaphore_signal(
            barrier, inc=1, device_id=(target(k), c), device_id_type=MESH
        )
    )
    pl.semaphore_signal(barrier, inc=1, device_id=(d, other), device_id_type=MESH)

    def right_side(f):
        return jnp.concatenate([to_f32(r_ref[f]), jnp.zeros((HALF, 128 - P_SIZE), F32)], 1)

    def enter(f, total):
        x = right_side(f)
        known[f, :HALF] = x.astype(BF16)
        return total + x * x

    stat_rows(lax.fori_loop(0, OWNED, enter, zero, unroll=8))
    pack_faces(right_side)
    pl.semaphore_wait(barrier, NDOM)

    each(lambda k: send_copy(k).start())
    across().start()
    spread(0)
    ahead = ELEMS // GROUP - 8

    def order(g):
        load(g).wait()
        relayout(staging.at[lax.rem(g, 2)], blocks, g * GROUP)

        @pl.when(g + 2 < ELEMS // GROUP)
        def _():
            load(g + 2).start()

        @pl.when(g >= ahead)
        def _():
            def one(j):
                k = (g - ahead) * 8 + j

                @pl.when(k > 0)
                def _():
                    arrive(k)

            loop(0, 8, one)

    loop(0, ELEMS // GROUP, order)
    halo_end()
    gathered(0)
    apply()
    start_norm = jnp.sqrt(total_of(0, 0) / ENTRIES + EPS)
    scale = 1.0 / to_rows(start_norm)

    def first_image(f, value, carry):
        u = value * scale
        b = (to_f32(known[f, :HALF]) * scale).astype(BF16)
        sums[f, HALF:] = u
        b1[f] = b
        b = to_f32(b)
        return carry[0] + b * b, carry[1] + b * u

    bb, bu = add_returned(first_image)
    local = lane_sum(bb)
    local = lane_sum(bu) / jnp.where(local > 0.0, local, 1.0)

    def square(f, total):
        off = sums[f, HALF:] - local * to_f32(b1[f])
        return total + off * off

    stat_rows(bb, bu, lax.fori_loop(0, OWNED, square, zero, unroll=8))
    spread(1)
    gathered(1)
    diagonal = total_of(1, 1) / ENTRIES
    bb = stat_of(1, 0)
    off = stat_of(1, 1) / jnp.where(bb > 0.0, bb, 1.0) - diagonal
    squares = jnp.sum(stat_of(1, 2) + off * off * bb, axis=0, keepdims=True)
    next_norm = jnp.sqrt(squares / ENTRIES + EPS)
    slope, scale2 = to_rows(diagonal), 1.0 / to_rows(next_norm)

    def second_basis(f):
        b = ((sums[f, HALF:] - slope * to_f32(b1[f])) * scale2).astype(BF16)
        known[f, :HALF] = b
        keep[f] = b

    loop(0, OWNED, second_basis, 8)
    pack_faces(lambda f: to_f32(keep[f]))
    across().start()
    each(lambda k: send_copy(k).start())
    basis = pltpu.make_async_copy(known.at[owned, low], basis_hbm, sem.at[1])
    basis.start()
    each(arrive, 3)
    halo_end()
    apply()

    def second_image(f, value, carry):
        sums[f, HALF:] = value
        return carry[0] + to_f32(b1[f]) * value, carry[1] + to_f32(known[f, :HALF]) * value

    stat_rows(*add_returned(second_image))
    spread(2)
    gathered(2)
    first_row, second_row = total_of(2, 0) / ENTRIES, total_of(2, 1) / ENTRIES
    h_ref[...] = jnp.zeros((8, 128), F32)
    for i, row in enumerate((start_norm, diagonal, next_norm, first_row, second_row)):
        h_ref[i : i + 1] = row
    p1, p2 = to_rows(first_row), to_rows(second_row)

    def last_vector(f):
        out = sums[f, HALF:] - p1 * to_f32(b1[f]) - p2 * to_f32(known[f, :HALF])
        keep[f] = out.astype(BF16)

    loop(0, OWNED, last_vector, 8)
    vector = pltpu.make_async_copy(keep, next_hbm, sem.at[2])
    vector.start()
    vector.wait()
    basis.wait()


def sems(n):
    return pltpu.SemaphoreType.DMA((n,))


def whole(scalars, r, blocks):
    faces, message = (OWNED, HALF, 128), (NDOM, WIRE, 128)
    vm = lambda shape, kind=BF16: pltpu.VMEM(shape, kind)
    return pl.pallas_call(
        whole_kernel,
        in_specs=[pl.BlockSpec(memory_space=pltpu.SMEM)] * len(scalars)
        + [pl.BlockSpec(memory_space=pltpu.VMEM), pl.BlockSpec(memory_space=pl.ANY)],
        out_specs=[pl.BlockSpec(memory_space=pl.ANY)] * 2
        + [pl.BlockSpec(memory_space=pltpu.VMEM)],
        out_shape=[
            jax.ShapeDtypeStruct(faces, BF16),
            jax.ShapeDtypeStruct(faces, BF16),
            jax.ShapeDtypeStruct((8, 128), F32),
        ],
        scratch_shapes=[
            vm((ELEMS, 256, 512)),
            vm((2 * OWNED, 2 * HALF, 128)),
            vm((4 * ELEMS + 1, 2 * HALF, 128), F32),
            vm(faces),
            vm(message), vm(message), vm(message),
            vm(faces), vm(faces), vm(faces),
            vm(message), vm(message), vm(message), vm(message),
            vm((8, 128), F32),
            vm((3, NDOM, 8, 128), F32),
            vm((2, 210, GROUP, 420)),
        ]
        + [sems(2)] + [sems(NDOM)] * 6 + [sems(PARTS)] * 2 + [sems(NDOM)] * 2 + [sems(4), sems(3)],
        compiler_params=pltpu.CompilerParams(
            collective_id=0, has_side_effects=True, vmem_limit_bytes=VMEM_LIMIT
        ),
    )(*scalars, r, blocks)


def latest(names, queries, before, usable, empty):
    j = jnp.arange(names.shape[0], dtype=jnp.int32)
    match = (names[None, :] == queries[:, None]) & (j[None, :] < before[:, None]) & usable[None, :]
    best = jnp.max(jnp.where(match, j[None, :], -1), axis=1)
    return jnp.where(best < 0, empty, best)


def body(adjoint_rhs, element_blocks, element_faces, send_faces):
    d = lax.axis_index("dom")
    faces = element_faces.reshape(-1)
    send = send_faces[0]
    slots = jnp.arange(2 * OWNED, dtype=jnp.int32)
    at = jnp.arange(faces.shape[0], dtype=jnp.int32)
    full = jnp.full((2 * OWNED,), 2 * OWNED, jnp.int32)
    every = jnp.ones((faces.shape[0],), bool)
    found = latest(
        faces, jnp.concatenate([faces, slots]), jnp.concatenate([at, full]), every, 4 * ELEMS
    )
    owned = slots[:OWNED]
    found2 = latest(
        send, jnp.concatenate([send, owned]), jnp.concatenate([owned, full[:OWNED]]),
        owned // SLOT != d, OWNED,
    )
    scalars = (
        send, faces, found[: 4 * ELEMS], found[4 * ELEMS :], found2[:OWNED], found2[OWNED:],
    )
    basis, vector, rows = whole(
        scalars, jnp.transpose(adjoint_rhs, (0, 2, 1)), jnp.transpose(element_blocks, (1, 0, 2))
    )
    out = lambda x: jnp.transpose(x[:, :, :P_SIZE], (0, 2, 1))
    return out(basis), out(vector), rows[:5, :HALF]


def solution(mesh):
    in_specs = (P("dom", None, "col"), P("dom", "col", None), P("dom", None), P("dom", None))
    out_specs = (P("dom", None, "col"), P("dom", None, "col"), P(None, "col"))
    return jax.shard_map(body, mesh=mesh, in_specs=in_specs, out_specs=out_specs, check_vma=False)
```

```python
import jax
import jax.numpy as jnp
from jax import lax
from jax.experimental import pallas as pl
from jax.experimental.pallas import tpu as pltpu
from jax.sharding import PartitionSpec as P

P_SIZE = 105
EPS = 1e-06
MESH = pl.DeviceIdType.MESH
NDOM = 64
ELEMS = 96
OWNED = 192
SLOT = 3
HALF = 32
WIRE = 80
STEP = 27
ENTRIES = float(NDOM * OWNED * P_SIZE)
F32 = jnp.float32
BF16 = jnp.bfloat16
INVERSE = 19
LAST = 4 * ELEMS
LAG = 4
VMEM_LIMIT = 67043328
GROUP = 8
PARTS = 8


def lanes(rows):
    return lax.broadcasted_iota(jnp.int32, (rows, 128), 1)


def rows_of(rows):
    return lax.broadcasted_iota(jnp.int32, (rows, 128), 0)


def pack(f0, f1, f2):
    lane = lanes(16)
    tail = f2[16:]
    out = []
    for j, part in enumerate((f0[:16], f0[16:], f1[:16], f1[16:], f2[:16])):
        moved = pltpu.roll(tail, 105 - 21 * j, 1)
        out.append(jnp.where(lane < 105, part, jnp.where(lane < 126, moved, 0.0)))
    return jnp.concatenate(out, axis=0)


def unpack(message):
    lane = lanes(16)
    tail = jnp.zeros((16, 128), F32)
    parts = []
    for j in range(5):
        part = message[16 * j : 16 * j + 16]
        moved = pltpu.roll(part, 128 - (105 - 21 * j), 1)
        tail = jnp.where((lane >= 21 * j) & (lane < 21 * j + 21), moved, tail)
        parts.append(jnp.where(lane < 105, part, 0.0))
    cat = lambda a, b: jnp.concatenate([a, b], axis=0)
    return cat(parts[0], parts[1]), cat(parts[2], parts[3]), cat(parts[4], tail)


def to_lanes(column, first):
    spread = jnp.where(rows_of(HALF) + first == lanes(HALF), column, 0.0)
    return jnp.sum(spread, axis=0, keepdims=True)


def to_rows(row):
    return jnp.sum(jnp.where(rows_of(HALF) == lanes(HALF), row, 0.0), axis=1, keepdims=True)


def lane_sum(x):
    return jnp.sum(x, axis=1, keepdims=True)


def relayout(a, o_ref, e0):
    group = GROUP
    at = pl.ds(e0, group)
    for s in range(2):
        for k in range(0, 105, 16):
            n = min(16, 105 - k)
            x = a[s * 105 + k : s * 105 + k + n]
            if n < 16:
                x = jnp.concatenate([x, jnp.zeros((16 - n, group, 420), x.dtype)], 0)
            y = jnp.swapaxes(x, 0, 1)
            for b in range(4):
                z = jnp.concatenate(
                    [y[:, :, 105 * b : 105 * b + 105], jnp.zeros((group, 16, 23), y.dtype)], -1
                )
                o_ref[at, s * 128 + k : s * 128 + k + 16, b * 128 : b * 128 + 128] = z
        o_ref[at, s * 128 + 112 : s * 128 + 128, :] = jnp.zeros((group, 16, 512), o_ref.dtype)


def offset(k):
    return lax.rem(k * STEP, NDOM)


def loop(first, last, body, unroll=1):
    def step(k, _):
        body(k)
        return 0

    lax.fori_loop(first, last, step, 0, unroll=unroll)


def each(body, unroll=1):
    loop(1, NDOM, body, unroll)


def remote(source, target, send, recv, d, c):
    return pltpu.make_async_remote_copy(
        source, target, send, recv, device_id=(d, c), device_id_type=MESH
    )


def to_f32(x):
    return x.astype(F32)


def whole_kernel(
    send_ref, faces_ref, found_ref, found2_ref, r_ref, a_hbm,
    basis_hbm, next_hbm, h_ref,
    blocks, known, sums, b1, wire, ghost, ghost2, keep, give, got, keepg, giveg, gotg, ret,
    stat, stats, staging,
    a_sem, hsend, hrecv, fsend, frecv, ssend, srecv, xsend, xrecv, rsend, rrecv, pair_sem, sem,
):
    d, c = lax.axis_index("dom"), lax.axis_index("col")
    other = 1 - c
    low, high = pl.ds(0, HALF), pl.ds(HALF, HALF)
    owned = pl.ds(0, OWNED)
    zero = jnp.zeros((HALF, 128), F32)

    def target(k):
        return lax.rem(d + offset(k), NDOM)

    def source(k):
        return lax.rem(d - offset(k) + NDOM, NDOM)

    def load(g):
        slot = lax.rem(g, 2)
        part = a_hbm.at[:, pl.ds(pl.multiple_of(g * GROUP, GROUP), GROUP), :]
        return pltpu.make_async_copy(part, staging.at[slot], a_sem.at[slot])

    def stat_copy(i, k):
        return remote(stat, stats.at[i, d], ssend.at[k], srecv.at[k], target(k), c)

    def spread(i):
        mine = pltpu.make_async_copy(stat, stats.at[i, d], sem.at[0])
        mine.start()
        each(lambda k: stat_copy(i, k).start())
        mine.wait()

    def gathered(i):
        each(lambda k: stat_copy(i, k).wait())

    def send_copy(k):
        return remote(wire.at[target(k)], ghost.at[d], hsend.at[k], hrecv.at[k], target(k), c)

    def forward(k):
        s = source(k)
        return remote(ghost.at[s], ghost2.at[s], fsend.at[k], frecv.at[k], d, other)

    def across():
        return remote(
            known.at[owned, low], known.at[owned, high], pair_sem.at[0], pair_sem.at[1], d, other
        )

    def cross(i):
        part = pl.ds(i * (NDOM // PARTS), NDOM // PARTS)
        return remote(giveg.at[part], gotg.at[part], xsend.at[i], xrecv.at[i], d, other)

    def give_copy():
        return remote(give, got, pair_sem.at[2], pair_sem.at[3], d, other)

    def back(k):
        return remote(keepg.at[k], ret.at[d], rsend.at[k], rrecv.at[k], target(k), c)

    def pack_faces(face):
        def step(p):
            faces = [face(send_ref[SLOT * p + s]) for s in range(SLOT)]
            wire[p] = pack(*faces).astype(BF16)

        return step

    def fill(s, source_ref, half):
        for j, face in enumerate(unpack(to_f32(source_ref[s]))):
            known[OWNED + SLOT * s + j, half * HALF : half * HALF + HALF] = face.astype(BF16)

    def arrive(k):
        send_copy(k).wait_recv()
        forward(k).start()
        fill(source(k), ghost, 0)

        @pl.when(k > LAG)
        def _():
            take_forward(k - LAG)

    def take_forward(k):
        forward(k).wait_recv()
        fill(source(k), ghost2, 1)

    def halo_end():
        loop(NDOM - LAG, NDOM, take_forward)

        def done(k):
            send_copy(k).wait_send()
            forward(k).wait_send()

        each(done)
        across().wait()

    def apply():
        first = 2 * c
        sums[4 * ELEMS] = jnp.zeros((2 * HALF, 128), F32)

        def element(e):
            at = 4 * e
            x = jnp.concatenate(
                [known[faces_ref[at + first]], known[faces_ref[at + first + 1]]], axis=1
            )
            y = jnp.dot(x, blocks[e], preferred_element_type=F32)
            for b in range(4):
                sums[at + b] = y[:, 128 * b : 128 * b + 128] + sums[found_ref[at + b]]

        loop(0, ELEMS, element, 8)
        size = NDOM // PARTS

        def part(i):
            def one(j):
                k = i * size + j
                p = target(k)
                t = [sums[found_ref[LAST + OWNED + SLOT * p + s]] for s in range(SLOT)]
                keepg[k] = pack(*(x[:HALF] for x in t)).astype(BF16)
                giveg[k] = pack(*(x[HALF:] for x in t)).astype(BF16)

            loop(0, size, one, 4)

        def pass_on(i):
            cross(i).wait_recv()

            def one(j):
                k = i * size + j
                keepg[k] = (to_f32(keepg[k]) + to_f32(gotg[k])).astype(BF16)

            loop(0, size, one, 4)

            def go(j):
                @pl.when(i + j > 0)
                def _():
                    back(i * size + j).start()

            loop(0, size, go)

        def stage(i):
            @pl.when(i < PARTS)
            def _():
                part(i)

            @pl.when(i >= 3)
            def _():
                pass_on(i - 3)

            @pl.when((i > 0) & (i <= PARTS))
            def _():
                cross(i - 1).start()

        loop(0, PARTS + 3, stage)

        def take(f):
            total = sums[found_ref[LAST + f]].astype(BF16)
            keep[f] = total[:HALF]
            give[f] = total[HALF:]

        loop(0, OWNED, take, 8)
        give_copy().start()

    def add_returned(image):
        sums[OWNED, :HALF] = zero

        def step(k):
            back(k).wait_recv()
            p = source(k)
            for s, face in enumerate(unpack(to_f32(ret[p]))):
                before = sums[found2_ref[SLOT * p + s], :HALF]
                sums[SLOT * k + s, :HALF] = face + before

        each(step, 3)
        each(lambda k: back(k).wait_send())
        loop(0, PARTS, lambda i: cross(i).wait_send())
        give_copy().wait()

        def own(f, carry):
            value = to_f32(keep[f]) + to_f32(got[f]) + sums[found2_ref[OWNED + f], :HALF]
            return image(f, value, carry)

        return lax.fori_loop(0, OWNED, own, (zero, zero), unroll=8)

    def stat_rows(*columns):
        stat[...] = sum(to_lanes(lane_sum(x), HALF * i) for i, x in enumerate(columns))

    def stat_of(i, row):
        found = stats[i, :, 0, :]
        return pltpu.roll(found, 128 - HALF * row, 1) if row else found

    def total_of(i, row):
        return jnp.sum(stat_of(i, row), axis=0, keepdims=True)

    load(0).start()
    load(1).start()
    barrier = pltpu.get_barrier_semaphore()
    each(
        lambda k: pl.semaphore_signal(
            barrier, inc=1, device_id=(target(k), c), device_id_type=MESH
        )
    )
    pl.semaphore_signal(barrier, inc=1, device_id=(d, other), device_id_type=MESH)

    def right_side(f):
        return jnp.concatenate([to_f32(r_ref[f]), jnp.zeros((HALF, 128 - P_SIZE), F32)], 1)

    def enter(f, total):
        x = right_side(f)
        known[f, :HALF] = x.astype(BF16)
        return total + x * x

    stat_rows(lax.fori_loop(0, OWNED, enter, zero, unroll=8))
    loop(0, NDOM, pack_faces(right_side), 4)
    pl.semaphore_wait(barrier, NDOM)

    each(lambda k: send_copy(k).start())
    across().start()
    spread(0)
    ahead = ELEMS // GROUP - 8

    def order(g):
        load(g).wait()
        relayout(staging.at[lax.rem(g, 2)], blocks, g * GROUP)

        @pl.when(g + 2 < ELEMS // GROUP)
        def _():
            load(g + 2).start()

        @pl.when(g >= ahead)
        def _():
            def one(j):
                k = (g - ahead) * 8 + j

                @pl.when(k > 0)
                def _():
                    arrive(k)

            loop(0, 8, one)

    loop(0, ELEMS // GROUP, order)
    halo_end()
    gathered(0)
    apply()
    start_norm = jnp.sqrt(total_of(0, 0) / ENTRIES + EPS)
    scale = 1.0 / to_rows(start_norm)

    def first_image(f, value, carry):
        u = value * scale
        b = (to_f32(known[f, :HALF]) * scale).astype(BF16)
        sums[f, HALF:] = u
        b1[f] = b
        b = to_f32(b)
        return carry[0] + b * b, carry[1] + b * u

    bb, bu = add_returned(first_image)
    local = lane_sum(bb)
    local = lane_sum(bu) / jnp.where(local > 0.0, local, 1.0)

    def square(f, total):
        off = sums[f, HALF:] - local * to_f32(b1[f])
        return total + off * off

    stat_rows(bb, bu, lax.fori_loop(0, OWNED, square, zero, unroll=8))
    spread(1)
    gathered(1)
    diagonal = total_of(1, 1) / ENTRIES
    bb = stat_of(1, 0)
    off = stat_of(1, 1) / jnp.where(bb > 0.0, bb, 1.0) - diagonal
    squares = jnp.sum(stat_of(1, 2) + off * off * bb, axis=0, keepdims=True)
    next_norm = jnp.sqrt(squares / ENTRIES + EPS)
    slope, scale2 = to_rows(diagonal), 1.0 / to_rows(next_norm)

    def second_basis(f):
        b = ((sums[f, HALF:] - slope * to_f32(b1[f])) * scale2).astype(BF16)
        known[f, :HALF] = b
        keep[f] = b

    loop(0, OWNED, second_basis, 8)
    across().start()
    pack_one = pack_faces(lambda f: to_f32(keep[f]))

    def send_some(i):
        @pl.when(i < 8)
        def _():
            loop(0, 8, lambda j: pack_one(target(8 * i + j)), 4)

        @pl.when(i > 0)
        def _():
            def go(j):
                @pl.when(8 * (i - 1) + j > 0)
                def _():
                    send_copy(8 * (i - 1) + j).start()

            loop(0, 8, go)

    loop(0, 9, send_some)
    basis = pltpu.make_async_copy(known.at[owned, low], basis_hbm, sem.at[1])
    basis.start()
    each(arrive, 3)
    halo_end()
    apply()

    def second_image(f, value, carry):
        sums[f, HALF:] = value
        return carry[0] + to_f32(b1[f]) * value, carry[1] + to_f32(known[f, :HALF]) * value

    stat_rows(*add_returned(second_image))
    spread(2)
    gathered(2)
    first_row, second_row = total_of(2, 0) / ENTRIES, total_of(2, 1) / ENTRIES
    h_ref[...] = jnp.zeros((8, 128), F32)
    for i, row in enumerate((start_norm, diagonal, next_norm, first_row, second_row)):
        h_ref[i : i + 1] = row
    p1, p2 = to_rows(first_row), to_rows(second_row)

    def last_vector(f):
        out = sums[f, HALF:] - p1 * to_f32(b1[f]) - p2 * to_f32(known[f, :HALF])
        keep[f] = out.astype(BF16)

    loop(0, OWNED, last_vector, 8)
    vector = pltpu.make_async_copy(keep, next_hbm, sem.at[2])
    vector.start()
    vector.wait()
    basis.wait()


def sems(n):
    return pltpu.SemaphoreType.DMA((n,))


def whole(scalars, r, blocks):
    faces, message = (OWNED, HALF, 128), (NDOM, WIRE, 128)
    vm = lambda shape, kind=BF16: pltpu.VMEM(shape, kind)
    return pl.pallas_call(
        whole_kernel,
        in_specs=[pl.BlockSpec(memory_space=pltpu.SMEM)] * len(scalars)
        + [pl.BlockSpec(memory_space=pltpu.VMEM), pl.BlockSpec(memory_space=pl.ANY)],
        out_specs=[pl.BlockSpec(memory_space=pl.ANY)] * 2
        + [pl.BlockSpec(memory_space=pltpu.VMEM)],
        out_shape=[
            jax.ShapeDtypeStruct(faces, BF16),
            jax.ShapeDtypeStruct(faces, BF16),
            jax.ShapeDtypeStruct((8, 128), F32),
        ],
        scratch_shapes=[
            vm((ELEMS, 256, 512)),
            vm((2 * OWNED, 2 * HALF, 128)),
            vm((4 * ELEMS + 1, 2 * HALF, 128), F32),
            vm(faces),
            vm(message), vm(message), vm(message),
            vm(faces), vm(faces), vm(faces),
            vm(message), vm(message), vm(message), vm(message),
            vm((1, 128), F32),
            vm((3, NDOM, 1, 128), F32),
            vm((2, 210, GROUP, 420)),
        ]
        + [sems(2)] + [sems(NDOM)] * 6 + [sems(PARTS)] * 2 + [sems(NDOM)] * 2 + [sems(4), sems(3)],
        compiler_params=pltpu.CompilerParams(
            collective_id=0, has_side_effects=True, vmem_limit_bytes=VMEM_LIMIT
        ),
    )(*scalars, r, blocks)


def latest(names, order, queries, before, usable, empty):
    match = (names[None, :] == queries[:, None]) & (order[None, :] < before[:, None])
    best = jnp.max(jnp.where(match & usable[None, :], order[None, :], -1), axis=1)
    return jnp.where(best < 0, empty, best)


def body(adjoint_rhs, element_blocks, element_faces, send_faces):
    d = lax.axis_index("dom")
    faces = element_faces.reshape(-1)
    send = send_faces[0]
    slots = jnp.arange(2 * OWNED, dtype=jnp.int32)
    at = jnp.arange(faces.shape[0], dtype=jnp.int32)
    full = jnp.full((2 * OWNED,), 2 * OWNED, jnp.int32)
    every = jnp.ones((faces.shape[0],), bool)
    found = latest(
        faces, at, jnp.concatenate([faces, slots]), jnp.concatenate([at, full]), every, 4 * ELEMS
    )
    owned = slots[:OWNED]
    partition = owned // SLOT
    arrival = SLOT * ((INVERSE * (d - partition + NDOM)) % NDOM) + owned % SLOT
    found2 = latest(
        send, arrival, jnp.concatenate([send, owned]), jnp.concatenate([arrival, full[:OWNED]]),
        partition != d, OWNED,
    )
    scalars = (send, faces, found, found2)
    basis, vector, rows = whole(
        scalars, jnp.transpose(adjoint_rhs, (0, 2, 1)), jnp.transpose(element_blocks, (1, 0, 2))
    )
    out = lambda x: jnp.transpose(x[:, :, :P_SIZE], (0, 2, 1))
    return out(basis), out(vector), rows[:5, :HALF]


def solution(mesh):
    in_specs = (P("dom", None, "col"), P("dom", "col", None), P("dom", None), P("dom", None))
    out_specs = (P("dom", None, "col"), P("dom", None, "col"), P(None, "col"))
    return jax.shard_map(body, mesh=mesh, in_specs=in_specs, out_specs=out_specs, check_vma=False)
```
